32 devices in a mesh: groups: 2 (over x), shot: 16 (over z, y, core).
Axes of the slice: x: 2, y: 2, z: 4, core: 2. Of those that a mesh axis runs over, the one named last changes fastest.
Arguments:
- blended: bfloat16 [32, 768, 512], P(('groups', 'shot')), parts along dimension 0, may hold values from -6 to 6
- partners: int32 [32], P(('groups', 'shot')), parts along dimension 0, may hold values from 0 to 15, as said below
- delays: int32 [32], P(('groups', 'shot')), parts along dimension 0, may hold values from 0 to 255
- time_taps: float32 [16, 5], replicated, may hold values from -2.5 to 2.5
- time_bias: float32 [16], replicated, may hold values from -0.5 to 0.5
- shot_taps: float32 [16, 5], replicated, may hold values from -2.5 to 2.5
- mix_weight: float32 [16, 16], replicated, may hold values from -1.5 to 1.5
- mix_bias: float32 [16], replicated, may hold values from -0.5 to 0.5
- up_taps: float32 [16, 5], replicated, may hold values from -0.875 to 0.875
Outputs:
- deblended: bfloat16 [32, 768, 512], P(('groups', 'shot')), parts along dimension 0
The draws below stay inside these ranges and needn't reach their ends.
There are 2 independent parts, one for each index of `groups`. The reference program is written for one: setup_inputs(seed, part) draws one part's arguments, and reference() takes and returns one part's arrays. A program takes and returns all parts, laid end to end along the dimension named above; an argument that names none is the same for every part. Nothing has to cross between parts.
Inputs may be any that keep to these rules, and one draw needn't show every extreme that they name: partners[s] is never s and lies at most 1 shots away from s in firing order; that distance is reached.
All inputs are finite; a program needn't handle non-finite values.
Results may differ from the reference program's by a relative error of at most 0.0053.
Values may be sent and summed in bfloat16 or wider, within the bound.
No kernel may reach another device: no remote copies, remote signals or barrier semaphores. Data moves between devices by JAX's collectives and lax.ppermute only.
A program may use at most 64 MiB of HBM per device.

```python
import jax
import jax.numpy as jnp
from jax import lax

SHOT_DEV = 1
RCV = 768
NT = 512
CH = 16
ITERS = 2
SHOTS = 16


def draw_partners(key, part):
    key_size = jax.random.fold_in(key, 11)
    key_sign = jax.random.fold_in(key, 12)
    position = jnp.arange(SHOTS, dtype=jnp.int32)
    distance = jax.random.randint(key_size, (SHOTS,), 1, SHOT_DEV + 1, dtype=jnp.int32)
    distance = jnp.where(position == 0, SHOT_DEV, distance)
    direction = jax.random.randint(key_sign, (SHOTS,), 0, 2, dtype=jnp.int32) * 2 - 1
    target = position + direction * distance
    target = jnp.where(target < 0, position + distance, target)
    target = jnp.where(target >= SHOTS, position - distance, target)
    return target.astype(jnp.int32)


def set_ends(array, key, smallest, high):
    shape = array.shape
    index_at = [jax.random.randint(jax.random.fold_in(key, axis), (), 0, shape[axis]) for axis in range(len(shape))]
    array = array.at[tuple(index_at)].set(smallest)
    longest = shape.index(max(shape))
    index_at[longest] = (index_at[longest] + 1) % shape[longest]
    return array.at[tuple(index_at)].set(high)


def block_levels(key, extent, shards, smallest, top_value):
    def one(axis_at, shards_of):
        steps = jax.random.uniform(jax.random.fold_in(jax.random.fold_in(key, 6), axis_at), (shards_of,), jnp.float32, smallest / len(shards), top_value / len(shards))
        return jnp.repeat(jnp.exp(steps), extent[axis_at] // shards_of).reshape((-1,) + (1,) * (len(extent) - axis_at - 1))

    level = one(*shards[0])
    for cut in shards[1:]:
        level = level * one(*cut)
    return level


def bell_draw(stream_key, extent, deviation, limit, shards=(), held_as=jnp.bfloat16):
    factor_of = block_levels(stream_key, extent, shards, -0.22, 0.18) if shards else 1.0
    drawn = jax.random.normal(stream_key, extent, jnp.float32) * deviation * factor_of
    return jnp.minimum(jnp.maximum(drawn, -limit), limit).astype(held_as)


def setup_inputs(seed: int = 0, part: int = 0) -> dict:
    keys = jax.random.split(jax.random.key(seed), 10)
    part_keys = jax.random.split(jax.random.fold_in(keys[9], part), 10)
    return {
        "blended": bell_draw(part_keys[0], (SHOTS, RCV, NT), 1.0, 6.0, ((0, 16),)),
        "partners": draw_partners(jax.random.fold_in(jax.random.fold_in(keys[9], part), 71), part),
        "delays": set_ends(jax.random.randint(part_keys[2], (SHOTS,), 0, NT // 2), jax.random.fold_in(part_keys[2], 1), 0, (NT // 2) - 1).astype(jnp.int32),
        "time_taps": bell_draw(keys[3], (CH, 5), 5 ** -0.5, 2.5, (), jnp.float32),
        "time_bias": jnp.clip(jax.random.uniform(keys[4], (CH,), jnp.float32, -0.5, 0.5), -0.5, 0.5),
        "shot_taps": bell_draw(keys[5], (CH, 5), 5 ** -0.5, 2.5, (), jnp.float32),
        "mix_weight": bell_draw(keys[6], (CH, CH), CH ** -0.5, 1.5, (), jnp.float32),
        "mix_bias": jnp.clip(jax.random.uniform(keys[7], (CH,), jnp.float32, -0.5, 0.5), -0.5, 0.5),
        "up_taps": bell_draw(keys[8], (CH, 5), (3 * CH) ** -0.5, 0.875, (), jnp.float32),
    }


def shifted_back(values):
    return jnp.pad(values[..., :-1], [(0, 0)] * (values.ndim - 1) + [(1, 0)])


def shifted_ahead(values):
    return jnp.pad(values[..., 1:], [(0, 0)] * (values.ndim - 1) + [(0, 1)])


def shot_neighbour(values, offset):
    if offset > 0:
        return jnp.pad(values[:, :, offset:, :], ((0, 0), (0, 0), (0, offset), (0, 0)))
    if offset < 0:
        return jnp.pad(values[:, :, :offset, :], ((0, 0), (0, 0), (-offset, 0), (0, 0)))
    return values


def denoise_images(images, time_taps, time_bias, shot_taps, mix_weight, mix_bias, up_taps):
    even_part = images[..., 0::2]
    odd_part = images[..., 1::2]
    planes = (shifted_back(even_part), shifted_back(odd_part), even_part, odd_part, shifted_ahead(even_part))
    total = jnp.zeros((images.shape[0], time_taps.shape[0], images.shape[1], even_part.shape[2]), jnp.float32)
    total = total + time_bias[None, :, None, None]
    for tap_index in range(5):
        total = total + time_taps[None, :, tap_index, None, None] * planes[tap_index][:, None]
    strided = jax.nn.relu(total)
    across = jnp.zeros_like(strided)
    for tap_index in range(5):
        across = across + shot_taps[None, :, tap_index, None, None] * shot_neighbour(strided, tap_index - 2)
    mixed_act = jnp.einsum("dc,gcsh->gdsh", mix_weight, across, precision=lax.Precision.HIGHEST)
    mixed_act = jax.nn.relu(mixed_act + mix_bias[None, :, None, None])
    projected = jnp.einsum("ck,gcsh->gksh", up_taps, mixed_act, precision=lax.Precision.HIGHEST)
    even_out = shifted_ahead(projected[:, 0]) + projected[:, 2] + shifted_back(projected[:, 4])
    odd_out = shifted_ahead(projected[:, 1]) + projected[:, 3]
    joined = jnp.stack([even_out, odd_out], axis=-1).reshape(images.shape)
    return images - joined


def delay_traces(traces, delays):
    lead = traces.shape[2] // 2
    padded = jnp.pad(traces, ((0, 0), (0, 0), (lead, 0)))

    def one_shot(trace_set, delay):
        return lax.dynamic_slice_in_dim(trace_set, (lead - delay).astype(jnp.int32), traces.shape[2], axis=1)

    return jax.vmap(one_shot)(padded, delays)


def reblend(denoised, record, partner_rows, delays):
    delayed = delay_traces(partner_rows, delays).astype(jnp.float32)
    value = denoised.astype(jnp.float32)
    return (value + 0.5 * (record.astype(jnp.float32) - value - delayed)).astype(jnp.bfloat16)


def reference(blended, partners, delays, time_taps, time_bias, shot_taps, mix_weight, mix_bias, up_taps):
    current = blended

    def denoise_group(group_block):
        cleaned = denoise_images(group_block.astype(jnp.float32), time_taps, time_bias, shot_taps, mix_weight, mix_bias, up_taps)
        return cleaned.astype(jnp.bfloat16)

    for iteration in range(ITERS):
        gathers = jnp.moveaxis(current, 1, 0).reshape(RCV // 16, 16, SHOTS, NT)
        denoised = lax.map(denoise_group, gathers).reshape(RCV, SHOTS, NT)
        denoised = jnp.moveaxis(denoised, 0, 1)
        partner_rows = jnp.take(denoised, partners, axis=0)
        current = reblend(denoised, blended, partner_rows, delays)
    return current
```

```python
import jax
import jax.numpy as jnp
from jax import lax
from jax.experimental import pallas as pl
from jax.experimental.pallas import tpu as pltpu
from jax.sharding import PartitionSpec as P

ITERS = 2
LANES = 128
UB = 8
HALVES = 2
TILES = 4
ONES_LANE = (96, 32)


def split_pair(value):
    high = value.astype(jnp.bfloat16)
    low = (value - high.astype(jnp.float32)).astype(jnp.bfloat16)
    return high, low


def prepare_kernel(lane_ref, mix_ref, up_ref, first_ref, mixing_ref, last_ref):
    for half in range(HALVES):
        row = lax.broadcasted_iota(jnp.int32, (LANES, TILES * LANES), 0)
        col = lax.broadcasted_iota(jnp.int32, (LANES, TILES * LANES), 1)
        sample = half * 32 + (col // LANES) * UB + col % UB
        taps = jnp.concatenate([lane_ref[...]] * TILES, axis=1)
        total = jnp.where(row == ONES_LANE[half], taps[5:6], 0.0)
        for k in range(5):
            total = total + jnp.where(row == ((2 * sample + k - 2) & (LANES - 1)), taps[k : k + 1], 0.0)
        high, low = split_pair(total)
        first_ref[half, :LANES, :] = high
        first_ref[half, LANES:, :] = low

        row = lax.broadcasted_iota(jnp.int32, (TILES * LANES, LANES), 0)
        col = lax.broadcasted_iota(jnp.int32, (TILES * LANES, LANES), 1)
        sample = half * 32 + (row // LANES) * UB + row % UB
        taps = jnp.concatenate([up_ref[...]] * TILES, axis=0)
        total = jnp.zeros((TILES * LANES, LANES), jnp.float32)
        for k in range(5):
            total = total + jnp.where(col == ((2 * sample + k - 2) & (LANES - 1)), taps[:, k : k + 1], 0.0)
        high, low = split_pair(total)
        last_ref[half, :, :LANES] = high
        last_ref[half, :, LANES:] = low

    row = lax.broadcasted_iota(jnp.int32, (LANES, LANES), 0)
    col = lax.broadcasted_iota(jnp.int32, (LANES, LANES), 1)
    high, low = split_pair(jnp.where(row % UB == col % UB, mix_ref[...], 0.0))
    mixing_ref[:LANES, :LANES] = high
    mixing_ref[LANES:, :LANES] = high
    mixing_ref[:LANES, LANES:] = low
    mixing_ref[LANES:, LANES:] = low


def prepare(time_taps, time_bias, shot_taps, mix_weight, mix_bias, up_taps):
    lanes = jnp.concatenate(
        [time_taps.T, time_bias[None], shot_taps.T, mix_bias[None], jnp.zeros((4, time_bias.shape[0]), jnp.float32)]
    )
    lanes = jnp.repeat(lanes, UB, axis=1)
    mix = jnp.repeat(jnp.repeat(mix_weight.T, UB, axis=0), UB, axis=1)
    up = jnp.repeat(up_taps, UB, axis=0)
    mats = pl.pallas_call(
        prepare_kernel,
        out_shape=(
            jax.ShapeDtypeStruct((HALVES, 2 * LANES, TILES * LANES), jnp.bfloat16),
            jax.ShapeDtypeStruct((2 * LANES, 2 * LANES), jnp.bfloat16),
            jax.ShapeDtypeStruct((HALVES, TILES * LANES, 2 * LANES), jnp.bfloat16),
        ),
        cost_estimate=pl.CostEstimate(flops=4_000_000, bytes_accessed=2_000_000, transcendentals=0),
    )(lanes, mix, up)
    return (lanes,) + mats


def deblend_kernel(
    shots, rcv, blocks,
    partner_ref, delay_ref, record_ref, lane_ref, first_ref, mixing_ref, last_ref, out_ref,
    current, strided, mixed_high, mixed_low, correction, denoised,
):
    rows = shots * rcv
    time_len = blocks * LANES
    halo = 2 * rcv
    zero_block = jnp.zeros((rows, LANES), jnp.bfloat16)
    current[:, :LANES] = zero_block
    current[:, (blocks + 1) * LANES :] = zero_block
    current[:, LANES : (blocks + 1) * LANES] = record_ref[...]
    strided[:halo, :] = jnp.zeros((halo, HALVES * TILES * LANES), jnp.float32)
    strided[halo + rows :, :] = jnp.zeros((halo, HALVES * TILES * LANES), jnp.float32)
    for half in range(HALVES):
        correction[half, :, :LANES] = jnp.zeros((rows, LANES), jnp.float32)
        correction[half, :, (blocks + 1) * LANES :] = jnp.zeros((rows, LANES), jnp.float32)
    lane = lax.broadcasted_iota(jnp.int32, (rows, LANES), 1)

    def one_block(block, carry):
        at = pl.multiple_of(block * LANES, LANES)
        before = current[:, pl.ds(at, LANES)]
        here = current[:, pl.ds(pl.multiple_of(at + LANES, LANES), LANES)]
        after = current[:, pl.ds(pl.multiple_of(at + 2 * LANES, LANES), LANES)]
        one = jnp.ones_like(here)
        windows = (
            jnp.where(lane >= LANES - 2, before, jnp.where(lane == ONES_LANE[0], one, here)),
            jnp.where(lane == 0, after, jnp.where(lane == ONES_LANE[1], one, here)),
        )
        for half in range(HALVES):
            window = jnp.concatenate([windows[half]] * 2, axis=1)
            total = jnp.dot(window, first_ref[half], preferred_element_type=jnp.float32)
            strided[halo : halo + rows, half * TILES * LANES : (half + 1) * TILES * LANES] = jnp.maximum(total, 0.0)

        def one_tile(tile, carry):
            at = pl.multiple_of(tile * LANES, LANES)
            across = None
            for k in range(5):
                term = strided[k * rcv : k * rcv + rows, pl.ds(at, LANES)] * lane_ref[6 + k : 7 + k, :]
                across = term if across is None else across + term
            high, low = split_pair(across)
            both = jnp.dot(jnp.concatenate([high, low], axis=1), mixing_ref[...], preferred_element_type=jnp.float32)
            mixed = jnp.maximum(both[:, :LANES] + both[:, LANES:] + lane_ref[11:12, :], 0.0)
            high, low = split_pair(mixed)
            mixed_high[:, pl.ds(at, LANES)] = high
            mixed_low[:, pl.ds(at, LANES)] = low
            return carry

        lax.fori_loop(0, HALVES * TILES, one_tile, 0)
        at = pl.multiple_of((block + 1) * LANES, LANES)
        for half in range(HALVES):
            span = slice(half * TILES * LANES, (half + 1) * TILES * LANES)
            both = jnp.dot(mixed_high[:, span], last_ref[half], preferred_element_type=jnp.float32)
            both = both + jnp.dot(mixed_low[:, span], last_ref[half], preferred_element_type=jnp.float32)
            correction[half, :, pl.ds(at, LANES)] = both[:, :LANES] + both[:, LANES:]
        return carry

    def one_iteration(iteration, carry):
        lax.fori_loop(0, blocks, one_block, 0)
        for block in range(blocks):
            at = (block + 1) * LANES
            low_half = jnp.where(lane < 96, correction[0, :, at : at + LANES], correction[0, :, at + LANES : at + 2 * LANES])
            high_half = jnp.where(lane >= 32, correction[1, :, at : at + LANES], correction[1, :, at - LANES : at])
            value = current[:, at : at + LANES].astype(jnp.float32) - (low_half + high_half)
            denoised[:, at - LANES : at] = value.astype(jnp.bfloat16)
        column = lax.broadcasted_iota(jnp.int32, (rcv, time_len), 1)

        def one_shot(shot, carry):
            delay = delay_ref[shot]
            here = pl.ds(pl.multiple_of(shot * rcv, rcv), rcv)
            there = pl.ds(pl.multiple_of(partner_ref[shot] * rcv, rcv), rcv)
            shifted = pltpu.roll(denoised[there, :].astype(jnp.float32), delay, 1)
            delayed = jnp.where(column >= delay, shifted, 0.0)
            value = denoised[here, :].astype(jnp.float32)
            record = record_ref[here, :].astype(jnp.float32)
            current[here, LANES : LANES + time_len] = (value + 0.5 * (record - value - delayed)).astype(jnp.bfloat16)
            return carry

        lax.fori_loop(0, shots, one_shot, 0)
        return carry

    lax.fori_loop(0, ITERS, one_iteration, 0)
    out_ref[...] = current[:, LANES : LANES + time_len]


def deblend(record, partners, delays, lanes, first, mixing, last, shots, rcv):
    rows, time_len = record.shape
    blocks = time_len // LANES
    wide = HALVES * TILES * LANES
    vmem = pl.BlockSpec(memory_space=pltpu.VMEM)
    smem = pl.BlockSpec(memory_space=pltpu.SMEM)

    def kernel(*refs):
        deblend_kernel(shots, rcv, blocks, *refs)

    return pl.pallas_call(
        kernel,
        out_shape=jax.ShapeDtypeStruct((rows, time_len), jnp.bfloat16),
        in_specs=[smem, smem, vmem, vmem, vmem, vmem, vmem],
        out_specs=vmem,
        scratch_shapes=[
            pltpu.VMEM((rows, (blocks + 2) * LANES), jnp.bfloat16),
            pltpu.VMEM((rows + 4 * rcv, wide), jnp.float32),
            pltpu.VMEM((rows, wide), jnp.bfloat16),
            pltpu.VMEM((rows, wide), jnp.bfloat16),
            pltpu.VMEM((HALVES, rows, (blocks + 2) * LANES), jnp.float32),
            pltpu.VMEM((rows, time_len), jnp.bfloat16),
        ],
        compiler_params=pltpu.CompilerParams(vmem_limit_bytes=48 << 20),
        cost_estimate=pl.CostEstimate(
            flops=ITERS * rows * time_len * 8 * 2 * 256 * 5, bytes_accessed=4 * rows * time_len, transcendentals=0
        ),
    )(partners, delays, record, lanes, first, mixing, last)


def body(blended, partners, delays, time_taps, time_bias, shot_taps, mix_weight, mix_bias, up_taps):
    shot_count, rcv_total, time_len = blended.shape
    peers = lax.axis_size("shot")
    shots = shot_count * peers
    rcv = rcv_total // peers
    padded = -(-rcv // 16) * 16
    orders = lax.all_gather(jnp.stack([partners, delays]), "shot", axis=1, tiled=True)
    mats = prepare(time_taps, time_bias, shot_taps, mix_weight, mix_bias, up_taps)
    pieces = jnp.moveaxis(blended.reshape(shot_count, peers, rcv, time_len), 1, 0)
    gathers = lax.all_to_all(pieces, "shot", split_axis=0, concat_axis=0, tiled=True).reshape(shots, rcv, time_len)
    gathers = jnp.pad(gathers, ((0, 0), (0, padded - rcv), (0, 0)))
    done = deblend(gathers.reshape(shots * padded, time_len), orders[0], orders[1], *mats, shots, padded)
    done = done.reshape(shots, padded, time_len)[:, :rcv]
    pieces = done.reshape(peers, shot_count, rcv, time_len)
    back = lax.all_to_all(pieces, "shot", split_axis=0, concat_axis=0, tiled=True)
    return jnp.moveaxis(back, 0, 1).reshape(shot_count, rcv_total, time_len)


def solution(mesh):
    placed = (
        P(("groups", "shot"), None, None),
        P(("groups", "shot")),
        P(("groups", "shot")),
        P(),
        P(),
        P(),
        P(),
        P(),
        P(),
    )
    return jax.shard_map(
        body,
        mesh=mesh,
        in_specs=placed,
        out_specs=P(("groups", "shot"), None, None),
        check_vma=False,
    )
```

```python
import jax
import jax.numpy as jnp
from jax import lax
from jax.experimental import pallas as pl
from jax.experimental.pallas import tpu as pltpu
from jax.sharding import PartitionSpec as P

ITERS = 2
LANES = 128
UB = 8
HALVES = 2
TILES = 4
ONES_LANE = (96, 32)


def split_pair(value):
    high = value.astype(jnp.bfloat16)
    low = (value - high.astype(jnp.float32)).astype(jnp.bfloat16)
    return high, low


def prepare_kernel(lane_ref, mix_ref, up_ref, first_ref, mixing_ref, last_ref):
    for half in range(HALVES):
        row = lax.broadcasted_iota(jnp.int32, (LANES, TILES * LANES), 0)
        col = lax.broadcasted_iota(jnp.int32, (LANES, TILES * LANES), 1)
        sample = half * 32 + (col // LANES) * UB + col % UB
        taps = jnp.concatenate([lane_ref[...]] * TILES, axis=1)
        total = jnp.where(row == ONES_LANE[half], taps[5:6], 0.0)
        for k in range(5):
            total = total + jnp.where(row == ((2 * sample + k - 2) & (LANES - 1)), taps[k : k + 1], 0.0)
        high, low = split_pair(total)
        first_ref[half, :LANES, :] = high
        first_ref[half, LANES:, :] = low

        row = lax.broadcasted_iota(jnp.int32, (TILES * LANES, LANES), 0)
        col = lax.broadcasted_iota(jnp.int32, (TILES * LANES, LANES), 1)
        sample = half * 32 + (row // LANES) * UB + row % UB
        taps = jnp.concatenate([up_ref[...]] * TILES, axis=0)
        total = jnp.zeros((TILES * LANES, LANES), jnp.float32)
        for k in range(5):
            total = total + jnp.where(col == ((2 * sample + k - 2) & (LANES - 1)), taps[:, k : k + 1], 0.0)
        high, low = split_pair(total)
        both = jnp.concatenate([high, low], axis=1)
        last_ref[half] = jnp.concatenate([both, both], axis=0)

    row = lax.broadcasted_iota(jnp.int32, (LANES, LANES), 0)
    col = lax.broadcasted_iota(jnp.int32, (LANES, LANES), 1)
    high, low = split_pair(jnp.where(row % UB == col % UB, mix_ref[...], 0.0))
    mixing_ref[:LANES, :LANES] = high
    mixing_ref[LANES:, :LANES] = high
    mixing_ref[:LANES, LANES:] = low
    mixing_ref[LANES:, LANES:] = low


def prepare(time_taps, time_bias, shot_taps, mix_weight, mix_bias, up_taps):
    lanes = jnp.concatenate(
        [time_taps.T, time_bias[None], shot_taps.T, mix_bias[None], jnp.zeros((4, time_bias.shape[0]), jnp.float32)]
    )
    lanes = jnp.repeat(lanes, UB, axis=1)
    mix = jnp.repeat(jnp.repeat(mix_weight.T, UB, axis=0), UB, axis=1)
    up = jnp.repeat(up_taps, UB, axis=0)
    mats = pl.pallas_call(
        prepare_kernel,
        out_shape=(
            jax.ShapeDtypeStruct((HALVES, 2 * LANES, TILES * LANES), jnp.bfloat16),
            jax.ShapeDtypeStruct((2 * LANES, 2 * LANES), jnp.bfloat16),
            jax.ShapeDtypeStruct((HALVES, 2 * TILES * LANES, 2 * LANES), jnp.bfloat16),
        ),
        compiler_params=pltpu.CompilerParams(vmem_limit_bytes=8 << 20),
        cost_estimate=pl.CostEstimate(flops=4_000_000, bytes_accessed=2_000_000, transcendentals=0),
    )(lanes, mix, up)
    return (lanes,) + mats


def deblend_kernel(
    shots, rcv, padded, stride, blocks,
    taken_ref, lane_ref, first_ref, mixing_ref, last_ref, out_ref,
    record, current, strided, correction, denoised, partner_ref, delay_ref,
):
    rows = shots * padded
    time_len = blocks * LANES
    base = rcv // 8 * 8
    marked = lax.broadcasted_iota(jnp.int32, (8, LANES), 0) == rcv - base
    place = lax.broadcasted_iota(jnp.int32, (8, LANES), 1)
    for shot in range(shots):
        order = taken_ref[shot * stride + base : shot * stride + base + 8, :LANES].astype(jnp.float32)
        partner_ref[shot] = jnp.sum(jnp.where(marked & (place == 0), order, 0.0)).astype(jnp.int32)
        delay_ref[shot] = jnp.sum(jnp.where(marked & (place == 1), order, 0.0)).astype(jnp.int32)
        piece = taken_ref[shot * stride : shot * stride + padded, :]
        record[shot * padded : (shot + 1) * padded, :] = piece
        current[shot * padded : (shot + 1) * padded, LANES : LANES + time_len] = piece
    zero_block = jnp.zeros((rows, LANES), jnp.bfloat16)
    current[:, :LANES] = zero_block
    current[:, (blocks + 1) * LANES :] = zero_block
    for half in range(HALVES):
        correction[half, :, :LANES] = jnp.zeros((rows, LANES), jnp.float32)
        correction[half, :, (blocks + 1) * LANES :] = jnp.zeros((rows, LANES), jnp.float32)
    lane = lax.broadcasted_iota(jnp.int32, (rows, LANES), 1)

    def one_block(block, carry):
        at = pl.multiple_of(block * LANES, LANES)
        middle = pl.multiple_of(at + LANES, LANES)
        before = current[:, pl.ds(at, LANES)]
        here = current[:, pl.ds(middle, LANES)]
        after = current[:, pl.ds(pl.multiple_of(at + 2 * LANES, LANES), LANES)]
        one = jnp.ones_like(here)
        windows = (
            jnp.where(lane >= LANES - 2, before, jnp.where(lane == ONES_LANE[0], one, here)),
            jnp.where(lane == 0, after, jnp.where(lane == ONES_LANE[1], one, here)),
        )

        def first_layer(half):
            window = jnp.concatenate([windows[half]] * 2, axis=1)
            total = jnp.dot(window, first_ref[half], preferred_element_type=jnp.float32)
            strided[:, half * TILES * LANES : (half + 1) * TILES * LANES] = jnp.maximum(total, 0.0)

        def one_tile(half, tile):
            span = slice((half * TILES + tile) * LANES, (half * TILES + tile + 1) * LANES)
            across = []
            for shot in range(shots):
                total = None
                for k in range(5):
                    source = shot + k - 2
                    if 0 <= source < shots:
                        term = strided[source * padded : (source + 1) * padded, span] * lane_ref[6 + k : 7 + k, :]
                        total = term if total is None else total + term
                across.append(total)
            high, low = split_pair(jnp.concatenate(across, axis=0))
            both = jnp.dot(jnp.concatenate([high, low], axis=1), mixing_ref[...], preferred_element_type=jnp.float32)
            return split_pair(jnp.maximum(both[:, :LANES] + both[:, LANES:] + lane_ref[11:12, :], 0.0))

        def last_layer(half, pairs):
            mixed = jnp.concatenate([pair[0] for pair in pairs] + [pair[1] for pair in pairs], axis=1)
            both = jnp.dot(mixed, last_ref[half], preferred_element_type=jnp.float32)
            correction[half, :, pl.ds(middle, LANES)] = both[:, :LANES] + both[:, LANES:]

        first_layer(0)
        pairs = [one_tile(0, 0)]
        first_layer(1)
        pairs = pairs + [one_tile(0, tile) for tile in range(1, TILES)]
        later = [one_tile(1, 0)]
        last_layer(0, pairs)
        later = later + [one_tile(1, tile) for tile in range(1, TILES)]
        last_layer(1, later)
        return carry

    def one_iteration(iteration, carry):
        lax.fori_loop(0, blocks, one_block, 0)
        for block in range(blocks):
            at = (block + 1) * LANES
            low_half = jnp.where(lane < 96, correction[0, :, at : at + LANES], correction[0, :, at + LANES : at + 2 * LANES])
            high_half = jnp.where(lane >= 32, correction[1, :, at : at + LANES], correction[1, :, at - LANES : at])
            value = current[:, at : at + LANES].astype(jnp.float32) - (low_half + high_half)
            denoised[:, at - LANES : at] = value.astype(jnp.bfloat16)
        column = lax.broadcasted_iota(jnp.int32, (padded, time_len), 1)

        def one_shot(shot, carry):
            delay = delay_ref[shot]
            here = pl.ds(pl.multiple_of(shot * padded, padded), padded)
            there = pl.ds(pl.multiple_of(partner_ref[shot] * padded, padded), padded)
            shifted = pltpu.roll(denoised[there, :].astype(jnp.float32), delay, 1)
            delayed = jnp.where(column >= delay, shifted, 0.0)
            value = denoised[here, :].astype(jnp.float32)
            original = record[here, :].astype(jnp.float32)
            current[here, LANES : LANES + time_len] = (value + 0.5 * (original - value - delayed)).astype(jnp.bfloat16)
            return carry

        lax.fori_loop(0, shots, one_shot, 0)
        return carry

    lax.fori_loop(0, ITERS, one_iteration, 0)
    out_ref[...] = current[:, LANES : LANES + time_len]


def deblend(taken, lanes, first, mixing, last, shots, rcv):
    total, time_len = taken.shape
    blocks = time_len // LANES
    padded = -(-rcv // 16) * 16
    rows = shots * padded
    wide = HALVES * TILES * LANES
    vmem = pl.BlockSpec(memory_space=pltpu.VMEM)

    def kernel(*refs):
        deblend_kernel(shots, rcv, padded, total // shots, blocks, *refs)

    return pl.pallas_call(
        kernel,
        out_shape=jax.ShapeDtypeStruct((rows, time_len), jnp.bfloat16),
        in_specs=[vmem] * 5,
        out_specs=vmem,
        scratch_shapes=[
            pltpu.VMEM((rows, time_len), jnp.bfloat16),
            pltpu.VMEM((rows, (blocks + 2) * LANES), jnp.bfloat16),
            pltpu.VMEM((rows, wide), jnp.float32),
            pltpu.VMEM((HALVES, rows, (blocks + 2) * LANES), jnp.float32),
            pltpu.VMEM((rows, time_len), jnp.bfloat16),
            pltpu.SMEM((shots,), jnp.int32),
            pltpu.SMEM((shots,), jnp.int32),
        ],
        compiler_params=pltpu.CompilerParams(vmem_limit_bytes=(8 << 20) + rows * 24576),
        cost_estimate=pl.CostEstimate(
            flops=ITERS * rows * time_len * 8 * 2 * 256 * 5, bytes_accessed=4 * rows * time_len, transcendentals=0
        ),
    )(taken, lanes, first, mixing, last)


def body(blended, partners, delays, time_taps, time_bias, shot_taps, mix_weight, mix_bias, up_taps):
    shot_count, rcv_total, time_len = blended.shape
    peers = lax.axis_size("shot")
    shots = shot_count * peers
    rcv = rcv_total // peers
    padded = -(-rcv // 16) * 16
    stride = padded + 8 if rcv == padded else padded
    mats = prepare(time_taps, time_bias, shot_taps, mix_weight, mix_bias, up_taps)
    pieces = jnp.moveaxis(blended.reshape(shot_count, peers, rcv, time_len), 1, 0)
    orders = jnp.stack([partners, delays], axis=1).astype(blended.dtype)
    orders = jnp.pad(orders[:, None, :], ((0, 0), (0, stride - rcv - 1), (0, time_len - 2)))
    orders = jnp.broadcast_to(orders[None], (peers,) + orders.shape)
    taken = lax.all_to_all(
        jnp.concatenate([pieces, orders], axis=2), "shot", split_axis=0, concat_axis=0, tiled=True
    ).reshape(shots * stride, time_len)
    done = deblend(taken, *mats, shots, rcv).reshape(shots, padded, time_len)[:, :rcv]
    pieces = done.reshape(peers, shot_count, rcv, time_len)
    back = lax.all_to_all(pieces, "shot", split_axis=0, concat_axis=0, tiled=True)
    return jnp.moveaxis(back, 0, 1).reshape(shot_count, rcv_total, time_len)


def solution(mesh):
    placed = (
        P(("groups", "shot"), None, None),
        P(("groups", "shot")),
        P(("groups", "shot")),
        P(),
        P(),
        P(),
        P(),
        P(),
        P(),
    )
    return jax.shard_map(
        body,
        mesh=mesh,
        in_specs=placed,
        out_specs=P(("groups", "shot"), None, None),
        check_vma=False,
    )
```

```python
import jax
import jax.numpy as jnp
from jax import lax
from jax.experimental import pallas as pl
from jax.experimental.pallas import tpu as pltpu
from jax.sharding import PartitionSpec as P

ITERS = 2
LANES = 128
SUBLANES = 8
UB = 8
HALVES = 2
TILES = 4
ONES_LANE = (96, 32)


def split_pair(value):
    high = value.astype(jnp.bfloat16)
    low = (value - high.astype(jnp.float32)).astype(jnp.bfloat16)
    return high, low


def prepare_kernel(lane_ref, mix_ref, up_ref, first_ref, mixing_ref, last_ref):
    for half in range(HALVES):
        row = lax.broadcasted_iota(jnp.int32, (LANES, TILES * LANES), 0)
        col = lax.broadcasted_iota(jnp.int32, (LANES, TILES * LANES), 1)
        sample = half * 32 + (col // LANES) * UB + col % UB
        taps = jnp.concatenate([lane_ref[...]] * TILES, axis=1)
        total = jnp.where(row == ONES_LANE[half], taps[5:6], 0.0)
        for k in range(5):
            total = total + jnp.where(row == ((2 * sample + k - 2) & (LANES - 1)), taps[k : k + 1], 0.0)
        high, low = split_pair(total)
        first_ref[half, :LANES, :] = high
        first_ref[half, LANES:, :] = low

        row = lax.broadcasted_iota(jnp.int32, (TILES * LANES, LANES), 0)
        col = lax.broadcasted_iota(jnp.int32, (TILES * LANES, LANES), 1)
        sample = half * 32 + (row // LANES) * UB + row % UB
        taps = jnp.concatenate([up_ref[...]] * TILES, axis=0)
        total = jnp.zeros((TILES * LANES, LANES), jnp.float32)
        for k in range(5):
            total = total + jnp.where(col == ((2 * sample + k - 2) & (LANES - 1)), taps[:, k : k + 1], 0.0)
        high, low = split_pair(total)
        both = jnp.concatenate([high, low], axis=1)
        last_ref[half] = jnp.concatenate([both, both], axis=0)

    row = lax.broadcasted_iota(jnp.int32, (LANES, LANES), 0)
    col = lax.broadcasted_iota(jnp.int32, (LANES, LANES), 1)
    high, low = split_pair(jnp.where(row % UB == col % UB, mix_ref[...], 0.0))
    mixing_ref[:LANES, :LANES] = high
    mixing_ref[LANES:, :LANES] = high
    mixing_ref[:LANES, LANES:] = low
    mixing_ref[LANES:, LANES:] = low


def prepare(time_taps, time_bias, shot_taps, mix_weight, mix_bias, up_taps):
    lanes = jnp.concatenate(
        [time_taps.T, time_bias[None], shot_taps.T, mix_bias[None], jnp.zeros((4, time_bias.shape[0]), jnp.float32)]
    )
    lanes = jnp.repeat(lanes, UB, axis=1)
    mix = jnp.repeat(jnp.repeat(mix_weight.T, UB, axis=0), UB, axis=1)
    up = jnp.repeat(up_taps, UB, axis=0)
    mats = pl.pallas_call(
        prepare_kernel,
        out_shape=(
            jax.ShapeDtypeStruct((HALVES, 2 * LANES, TILES * LANES), jnp.bfloat16),
            jax.ShapeDtypeStruct((2 * LANES, 2 * LANES), jnp.bfloat16),
            jax.ShapeDtypeStruct((HALVES, 2 * TILES * LANES, 2 * LANES), jnp.bfloat16),
        ),
        compiler_params=pltpu.CompilerParams(vmem_limit_bytes=8 << 20),
        cost_estimate=pl.CostEstimate(flops=4_000_000, bytes_accessed=2_000_000, transcendentals=0),
    )(lanes, mix, up)
    return (lanes,) + mats


def deblend_kernel(
    shots, padded, blocks,
    taken_ref, lane_ref, first_ref, mixing_ref, last_ref, out_ref,
    record, current, strided, correction, denoised, partner_ref, delay_ref,
):
    rows = shots * padded
    time_len = blocks * LANES
    tiles = padded // SUBLANES * blocks
    lane = lax.broadcasted_iota(jnp.int32, (SUBLANES, LANES), 1)
    first_row = lax.broadcasted_iota(jnp.int32, (SUBLANES, LANES), 0) == 0
    for shot in range(shots):
        order = taken_ref[shot, tiles].astype(jnp.float32)
        partner_ref[shot] = jnp.sum(jnp.where(first_row & (lane == 0), order, 0.0)).astype(jnp.int32)
        delay_ref[shot] = jnp.sum(jnp.where(first_row & (lane == 1), order, 0.0)).astype(jnp.int32)
        for block in range(blocks):
            pieces = [taken_ref[shot, group * blocks + block] for group in range(padded // SUBLANES)]
            piece = jnp.concatenate(pieces, axis=0)
            place = slice(shot * padded, (shot + 1) * padded)
            record[place, block * LANES : (block + 1) * LANES] = piece
            current[place, (block + 1) * LANES : (block + 2) * LANES] = piece
    zero_block = jnp.zeros((rows, LANES), jnp.bfloat16)
    current[:, :LANES] = zero_block
    current[:, (blocks + 1) * LANES :] = zero_block
    for half in range(HALVES):
        correction[half, :, :LANES] = jnp.zeros((rows, LANES), jnp.float32)
        correction[half, :, (blocks + 1) * LANES :] = jnp.zeros((rows, LANES), jnp.float32)
    lane = lax.broadcasted_iota(jnp.int32, (rows, LANES), 1)

    def one_block(block):
        at = block * LANES
        middle = at + LANES
        before = current[:, at : at + LANES]
        here = current[:, middle : middle + LANES]
        after = current[:, middle + LANES : middle + 2 * LANES]
        one = jnp.ones_like(here)
        windows = (
            jnp.where(lane >= LANES - 2, before, jnp.where(lane == ONES_LANE[0], one, here)),
            jnp.where(lane == 0, after, jnp.where(lane == ONES_LANE[1], one, here)),
        )

        def first_layer(half):
            window = jnp.concatenate([windows[half]] * 2, axis=1)
            total = jnp.dot(window, first_ref[half], preferred_element_type=jnp.float32)
            strided[:, half * TILES * LANES : (half + 1) * TILES * LANES] = jnp.maximum(total, 0.0)

        def one_tile(half, tile):
            span = slice((half * TILES + tile) * LANES, (half * TILES + tile + 1) * LANES)
            across = []
            for shot in range(shots):
                total = None
                for k in range(5):
                    source = shot + k - 2
                    if 0 <= source < shots:
                        term = strided[source * padded : (source + 1) * padded, span] * lane_ref[6 + k : 7 + k, :]
                        total = term if total is None else total + term
                across.append(total)
            high, low = split_pair(jnp.concatenate(across, axis=0))
            both = jnp.dot(jnp.concatenate([high, low], axis=1), mixing_ref[...], preferred_element_type=jnp.float32)
            return split_pair(jnp.maximum(both[:, :LANES] + both[:, LANES:] + lane_ref[11:12, :], 0.0))

        def last_layer(half, pairs):
            mixed = jnp.concatenate([pair[0] for pair in pairs] + [pair[1] for pair in pairs], axis=1)
            both = jnp.dot(mixed, last_ref[half], preferred_element_type=jnp.float32)
            correction[half, :, middle : middle + LANES] = both[:, :LANES] + both[:, LANES:]

        first_layer(0)
        pairs = [one_tile(0, 0)]
        first_layer(1)
        pairs = pairs + [one_tile(0, tile) for tile in range(1, TILES)]
        later = [one_tile(1, 0)]
        last_layer(0, pairs)
        later = later + [one_tile(1, tile) for tile in range(1, TILES)]
        last_layer(1, later)

    def one_iteration(iteration, carry):
        for block in range(blocks):
            one_block(block)
        for block in range(blocks):
            at = (block + 1) * LANES
            low_half = jnp.where(lane < 96, correction[0, :, at : at + LANES], correction[0, :, at + LANES : at + 2 * LANES])
            high_half = jnp.where(lane >= 32, correction[1, :, at : at + LANES], correction[1, :, at - LANES : at])
            value = current[:, at : at + LANES].astype(jnp.float32) - (low_half + high_half)
            denoised[:, at - LANES : at] = value.astype(jnp.bfloat16)
        column = lax.broadcasted_iota(jnp.int32, (padded, time_len), 1)

        def one_shot(shot, carry):
            delay = delay_ref[shot]
            here = pl.ds(pl.multiple_of(shot * padded, padded), padded)
            there = pl.ds(pl.multiple_of(partner_ref[shot] * padded, padded), padded)
            shifted = pltpu.roll(denoised[there, :].astype(jnp.float32), delay, 1)
            delayed = jnp.where(column >= delay, shifted, 0.0)
            value = denoised[here, :].astype(jnp.float32)
            original = record[here, :].astype(jnp.float32)
            current[here, LANES : LANES + time_len] = (value + 0.5 * (original - value - delayed)).astype(jnp.bfloat16)
            return carry

        lax.fori_loop(0, shots, one_shot, 0, unroll=4)
        return carry

    lax.fori_loop(0, ITERS, one_iteration, 0)
    out_ref[...] = current[:, LANES : LANES + time_len]


def deblend(taken, lanes, first, mixing, last, shots, padded, time_len):
    blocks = time_len // LANES
    rows = shots * padded
    wide = HALVES * TILES * LANES
    vmem = pl.BlockSpec(memory_space=pltpu.VMEM)

    def kernel(*refs):
        deblend_kernel(shots, padded, blocks, *refs)

    return pl.pallas_call(
        kernel,
        out_shape=jax.ShapeDtypeStruct((rows, time_len), jnp.bfloat16),
        in_specs=[vmem] * 5,
        out_specs=vmem,
        scratch_shapes=[
            pltpu.VMEM((rows, time_len), jnp.bfloat16),
            pltpu.VMEM((rows, (blocks + 2) * LANES), jnp.bfloat16),
            pltpu.VMEM((rows, wide), jnp.float32),
            pltpu.VMEM((HALVES, rows, (blocks + 2) * LANES), jnp.float32),
            pltpu.VMEM((rows, time_len), jnp.bfloat16),
            pltpu.SMEM((shots,), jnp.int32),
            pltpu.SMEM((shots,), jnp.int32),
        ],
        compiler_params=pltpu.CompilerParams(vmem_limit_bytes=(8 << 20) + rows * 24576),
        cost_estimate=pl.CostEstimate(
            flops=ITERS * rows * time_len * 8 * 2 * 256 * 5, bytes_accessed=4 * rows * time_len, transcendentals=0
        ),
    )(taken, lanes, first, mixing, last)


def body(blended, partners, delays, time_taps, time_bias, shot_taps, mix_weight, mix_bias, up_taps):
    shot_count, rcv_total, time_len = blended.shape
    peers = lax.axis_size("shot")
    shots = shot_count * peers
    rcv = rcv_total // peers
    padded = -(-rcv // SUBLANES) * SUBLANES
    blocks = time_len // LANES
    mats = prepare(time_taps, time_bias, shot_taps, mix_weight, mix_bias, up_taps)
    pieces = jnp.moveaxis(blended.reshape(shot_count, peers, rcv, time_len), 1, 0)
    pieces = jnp.pad(pieces, ((0, 0), (0, 0), (0, padded - rcv), (0, 0)))
    pieces = jnp.swapaxes(
        pieces.reshape(peers, shot_count, padded // SUBLANES, SUBLANES, blocks, LANES), 3, 4
    ).reshape(peers, shot_count, padded // SUBLANES * blocks, SUBLANES, LANES)
    orders = jnp.stack([partners, delays], axis=1).astype(blended.dtype)
    orders = jnp.pad(orders[:, None, None, :], ((0, 0), (0, 0), (0, SUBLANES - 1), (0, LANES - 2)))
    orders = jnp.broadcast_to(orders[None], (peers,) + orders.shape)
    taken = lax.all_to_all(
        jnp.concatenate([pieces, orders], axis=2), "shot", split_axis=0, concat_axis=0, tiled=True
    )
    taken = taken.reshape((shots,) + taken.shape[2:])
    done = deblend(taken, *mats, shots, padded, time_len).reshape(shots, padded, time_len)[:, :rcv]
    pieces = done.reshape(peers, shot_count, rcv, time_len)
    back = lax.all_to_all(pieces, "shot", split_axis=0, concat_axis=0, tiled=True)
    return jnp.moveaxis(back, 0, 1).reshape(shot_count, rcv_total, time_len)


def solution(mesh):
    placed = (
        P(("groups", "shot"), None, None),
        P(("groups", "shot")),
        P(("groups", "shot")),
        P(),
        P(),
        P(),
        P(),
        P(),
        P(),
    )
    return jax.shard_map(
        body,
        mesh=mesh,
        in_specs=placed,
        out_specs=P(("groups", "shot"), None, None),
        check_vma=False,
    )
```

```python
import jax
import jax.numpy as jnp
from jax import lax
from jax.experimental import pallas as pl
from jax.experimental.pallas import tpu as pltpu
from jax.sharding import PartitionSpec as P

ITERS = 2
LANES = 128
SUBLANES = 8
UB = 8
PARTS = 2
HALVES = 2
TILES = 4
ONES_LANE = (96, 32)


def split_pair(value):
    high = value.astype(jnp.bfloat16)
    low = (value - high.astype(jnp.float32)).astype(jnp.bfloat16)
    return high, low


def prepare_kernel(lane_ref, mix_ref, up_ref, first_ref, mixing_ref, last_ref):
    for half in range(HALVES):
        row = lax.broadcasted_iota(jnp.int32, (LANES, TILES * LANES), 0)
        col = lax.broadcasted_iota(jnp.int32, (LANES, TILES * LANES), 1)
        sample = half * 32 + (col // LANES) * UB + col % UB
        taps = jnp.concatenate([lane_ref[...]] * TILES, axis=1)
        total = jnp.where(row == ONES_LANE[half], taps[5:6], 0.0)
        for k in range(5):
            total = total + jnp.where(row == ((2 * sample + k - 2) & (LANES - 1)), taps[k : k + 1], 0.0)
        high, low = split_pair(total)
        first_ref[half, :LANES, :] = high
        first_ref[half, LANES:, :] = low

        row = lax.broadcasted_iota(jnp.int32, (TILES * LANES, LANES), 0)
        col = lax.broadcasted_iota(jnp.int32, (TILES * LANES, LANES), 1)
        sample = half * 32 + (row // LANES) * UB + row % UB
        taps = jnp.concatenate([up_ref[...]] * TILES, axis=0)
        total = jnp.zeros((TILES * LANES, LANES), jnp.float32)
        for k in range(5):
            total = total + jnp.where(col == ((2 * sample + k - 2) & (LANES - 1)), taps[:, k : k + 1], 0.0)
        high, low = split_pair(total)
        both = jnp.concatenate([high, low], axis=1)
        last_ref[half] = jnp.concatenate([both, both], axis=0)

    row = lax.broadcasted_iota(jnp.int32, (LANES, LANES), 0)
    col = lax.broadcasted_iota(jnp.int32, (LANES, LANES), 1)
    high, low = split_pair(jnp.where(row % UB == col % UB, mix_ref[...], 0.0))
    mixing_ref[:LANES, :LANES] = high
    mixing_ref[LANES:, :LANES] = high
    mixing_ref[:LANES, LANES:] = low
    mixing_ref[LANES:, LANES:] = low


def prepare(time_taps, time_bias, shot_taps, mix_weight, mix_bias, up_taps, time_len):
    lanes = jnp.concatenate(
        [time_taps.T, time_bias[None], shot_taps.T, mix_bias[None], jnp.zeros((4, time_bias.shape[0]), jnp.float32)]
    )
    lanes = jnp.repeat(lanes, UB, axis=1)
    mix = jnp.repeat(jnp.repeat(mix_weight.T, UB, axis=0), UB, axis=1)
    up = jnp.repeat(up_taps, UB, axis=0)
    level = jnp.sum(up_taps * mix_bias[:, None], axis=0)
    sample = jnp.arange(time_len)
    reached = [(sample + 2 - k) % 2 == 0 for k in range(5)]
    reached = [fits & (sample + 2 >= k) & (sample + 2 - k < time_len) for k, fits in enumerate(reached)]
    level = sum(jnp.where(fits, level[k], 0.0) for k, fits in enumerate(reached))[None]
    mats = pl.pallas_call(
        prepare_kernel,
        out_shape=(
            jax.ShapeDtypeStruct((HALVES, 2 * LANES, TILES * LANES), jnp.bfloat16),
            jax.ShapeDtypeStruct((2 * LANES, 2 * LANES), jnp.bfloat16),
            jax.ShapeDtypeStruct((HALVES, 2 * TILES * LANES, 2 * LANES), jnp.bfloat16),
        ),
        compiler_params=pltpu.CompilerParams(vmem_limit_bytes=8 << 20),
        cost_estimate=pl.CostEstimate(flops=4_000_000, bytes_accessed=2_000_000, transcendentals=0),
    )(lanes, mix, up)
    return (level, lanes) + tuple(mats)


def deblend_kernel(
    shots, padded, blocks,
    taken_ref, level_ref, lane_ref, first_ref, mixing_ref, last_ref, out_ref,
    record, current, strided, correction, denoised, partner_ref, delay_ref,
):
    rows = shots * padded
    time_len = blocks * LANES
    tiles = padded // SUBLANES * blocks
    lane = lax.broadcasted_iota(jnp.int32, (SUBLANES, LANES), 1)
    first_row = lax.broadcasted_iota(jnp.int32, (SUBLANES, LANES), 0) == 0
    for shot in range(shots):
        order = taken_ref[shot, tiles].astype(jnp.float32)
        partner_ref[shot] = jnp.sum(jnp.where(first_row & (lane == 0), order, 0.0)).astype(jnp.int32)
        delay_ref[shot] = jnp.sum(jnp.where(first_row & (lane == 1), order, 0.0)).astype(jnp.int32)
        for block in range(blocks):
            pieces = [taken_ref[shot, group * blocks + block] for group in range(padded // SUBLANES)]
            piece = jnp.concatenate(pieces, axis=0)
            place = slice(shot * padded, (shot + 1) * padded)
            record[place, block * LANES : (block + 1) * LANES] = piece
            current[place, (block + 1) * LANES : (block + 2) * LANES] = piece
    zero_block = jnp.zeros((rows, LANES), jnp.bfloat16)
    current[:, :LANES] = zero_block
    current[:, (blocks + 1) * LANES :] = zero_block
    for half in range(HALVES):
        correction[half, :, :LANES] = jnp.zeros((rows, LANES), jnp.float32)
        correction[half, :, (blocks + 1) * LANES :] = jnp.zeros((rows, LANES), jnp.float32)
    lane = lax.broadcasted_iota(jnp.int32, (rows, LANES), 1)

    def windows_of(block):
        at = block * LANES
        middle = at + LANES
        before = current[:, at : at + LANES]
        here = current[:, middle : middle + LANES]
        after = current[:, middle + LANES : middle + 2 * LANES]
        one = jnp.ones_like(here)
        return (
            jnp.where(lane >= LANES - 2, before, jnp.where(lane == ONES_LANE[0], one, here)),
            jnp.where(lane == 0, after, jnp.where(lane == ONES_LANE[1], one, here)),
        )

    def first_layer(block, half, pair):
        span = slice(pair * 2 * LANES, (pair + 1) * 2 * LANES)
        window = jnp.concatenate([windows[block][half]] * 2, axis=1)
        total = jnp.dot(window, first_ref[half, :, span], preferred_element_type=jnp.float32)
        start = half * TILES * LANES
        strided[:, start + span.start : start + span.stop] = jnp.maximum(total, 0.0)

    def shot_filter(half, tile):
        span = slice((half * TILES + tile) * LANES, (half * TILES + tile + 1) * LANES)
        across = []
        for shot in range(shots):
            total = None
            for k in range(5):
                source = shot + k - 2
                if 0 <= source < shots:
                    term = strided[source * padded : (source + 1) * padded, span] * lane_ref[6 + k : 7 + k, :]
                    total = term if total is None else total + term
            across.append(total)
        return split_pair(jnp.concatenate(across, axis=0))

    def mix(pair):
        both = jnp.dot(jnp.concatenate(pair, axis=1), mixing_ref[...], preferred_element_type=jnp.float32)
        return split_pair(jnp.maximum(both[:, :LANES] + both[:, LANES:], -lane_ref[11:12, :]))

    def last_layer(block, half, pairs, part):
        span = slice(part * rows // PARTS, (part + 1) * rows // PARTS)
        mixed = [pair[0][span] for pair in pairs] + [pair[1][span] for pair in pairs]
        both = jnp.dot(jnp.concatenate(mixed, axis=1), last_ref[half], preferred_element_type=jnp.float32)
        correction[half, span, (block + 1) * LANES : (block + 2) * LANES] = both[:, :LANES] + both[:, LANES:]

    windows = {}

    def one_iteration(iteration, carry):
        halves = [(block, half) for block in range(blocks) for half in range(HALVES)]
        windows[0] = windows_of(0)
        for pair in range(TILES // 2):
            first_layer(0, 0, pair)
        before = []
        for number, (block, half) in enumerate(halves):
            after = []
            if number + 1 < len(halves):
                following = halves[number + 1]
                if following[0] not in windows:
                    windows[following[0]] = windows_of(following[0])
                after = [lambda pair=pair, at=following: first_layer(*at, pair) for pair in range(TILES // 2)]
            beside = []
            while before or after:
                beside = beside + before[:1] + after[:1]
                before, after = before[1:], after[1:]
            pairs = []
            for tile in range(TILES):
                filtered = shot_filter(half, tile)
                share = -(-len(beside) // (TILES - tile))
                for step in beside[:share]:
                    step()
                beside = beside[share:]
                pairs.append(mix(filtered))
            before = [
                lambda at=(block, half), pairs=pairs, part=part: last_layer(*at, pairs, part) for part in range(PARTS)
            ]
        for step in before:
            step()
        windows.clear()
        for block in range(blocks):
            at = (block + 1) * LANES
            low_half = jnp.where(lane < 96, correction[0, :, at : at + LANES], correction[0, :, at + LANES : at + 2 * LANES])
            high_half = jnp.where(lane >= 32, correction[1, :, at : at + LANES], correction[1, :, at - LANES : at])
            total = low_half + high_half + level_ref[:, at - LANES : at]
            value = current[:, at : at + LANES].astype(jnp.float32) - total
            denoised[:, at - LANES : at] = value.astype(jnp.bfloat16)
        column = lax.broadcasted_iota(jnp.int32, (padded, time_len), 1)

        def one_shot(shot, carry):
            delay = delay_ref[shot]
            here = pl.ds(pl.multiple_of(shot * padded, padded), padded)
            there = pl.ds(pl.multiple_of(partner_ref[shot] * padded, padded), padded)
            shifted = pltpu.roll(denoised[there, :].astype(jnp.float32), delay, 1)
            delayed = jnp.where(column >= delay, shifted, 0.0)
            value = denoised[here, :].astype(jnp.float32)
            original = record[here, :].astype(jnp.float32)
            current[here, LANES : LANES + time_len] = (value + 0.5 * (original - value - delayed)).astype(jnp.bfloat16)
            return carry

        lax.fori_loop(0, shots, one_shot, 0, unroll=4)
        return carry

    lax.fori_loop(0, ITERS, one_iteration, 0)
    out_ref[...] = current[:, LANES : LANES + time_len]


def deblend(taken, level, lanes, first, mixing, last, shots, padded, time_len):
    blocks = time_len // LANES
    rows = shots * padded
    wide = HALVES * TILES * LANES
    vmem = pl.BlockSpec(memory_space=pltpu.VMEM)

    def kernel(*refs):
        deblend_kernel(shots, padded, blocks, *refs)

    return pl.pallas_call(
        kernel,
        out_shape=jax.ShapeDtypeStruct((rows, time_len), jnp.bfloat16),
        in_specs=[vmem] * 6,
        out_specs=vmem,
        scratch_shapes=[
            pltpu.VMEM((rows, time_len), jnp.bfloat16),
            pltpu.VMEM((rows, (blocks + 2) * LANES), jnp.bfloat16),
            pltpu.VMEM((rows, wide), jnp.float32),
            pltpu.VMEM((HALVES, rows, (blocks + 2) * LANES), jnp.float32),
            pltpu.VMEM((rows, time_len), jnp.bfloat16),
            pltpu.SMEM((shots,), jnp.int32),
            pltpu.SMEM((shots,), jnp.int32),
        ],
        compiler_params=pltpu.CompilerParams(vmem_limit_bytes=(8 << 20) + rows * 24576),
        cost_estimate=pl.CostEstimate(
            flops=ITERS * rows * time_len * 8 * 2 * 256 * 5, bytes_accessed=4 * rows * time_len, transcendentals=0
        ),
    )(taken, level, lanes, first, mixing, last)


def body(blended, partners, delays, time_taps, time_bias, shot_taps, mix_weight, mix_bias, up_taps):
    shot_count, rcv_total, time_len = blended.shape
    peers = lax.axis_size("shot")
    shots = shot_count * peers
    rcv = rcv_total // peers
    padded = -(-rcv // SUBLANES) * SUBLANES
    blocks = time_len // LANES
    mats = prepare(time_taps, time_bias, shot_taps, mix_weight, mix_bias, up_taps, time_len)
    pieces = jnp.moveaxis(blended.reshape(shot_count, peers, rcv, time_len), 1, 0)
    pieces = jnp.pad(pieces, ((0, 0), (0, 0), (0, padded - rcv), (0, 0)))
    pieces = jnp.swapaxes(
        pieces.reshape(peers, shot_count, padded // SUBLANES, SUBLANES, blocks, LANES), 3, 4
    ).reshape(peers, shot_count, padded // SUBLANES * blocks, SUBLANES, LANES)
    orders = jnp.stack([partners, delays], axis=1).astype(blended.dtype)
    orders = jnp.pad(orders[:, None, None, :], ((0, 0), (0, 0), (0, SUBLANES - 1), (0, LANES - 2)))
    orders = jnp.broadcast_to(orders[None], (peers,) + orders.shape)
    taken = lax.all_to_all(
        jnp.concatenate([pieces, orders], axis=2), "shot", split_axis=0, concat_axis=0, tiled=True
    )
    taken = taken.reshape((shots,) + taken.shape[2:])
    done = deblend(taken, *mats, shots, padded, time_len).reshape(shots, padded, time_len)[:, :rcv]
    pieces = done.reshape(peers, shot_count, rcv, time_len)
    back = lax.all_to_all(pieces, "shot", split_axis=0, concat_axis=0, tiled=True)
    return jnp.moveaxis(back, 0, 1).reshape(shot_count, rcv_total, time_len)


def solution(mesh):
    placed = (
        P(("groups", "shot"), None, None),
        P(("groups", "shot")),
        P(("groups", "shot")),
        P(),
        P(),
        P(),
        P(),
        P(),
        P(),
    )
    return jax.shard_map(
        body,
        mesh=mesh,
        in_specs=placed,
        out_specs=P(("groups", "shot"), None, None),
        check_vma=False,
    )
```
